32 devices in a mesh: img: 16 (over z, y, x), ref: 2 (over core).
Axes of the slice: x: 2, y: 2, z: 4, core: 2. Of those that a mesh axis runs over, the one named last changes fastest.
Arguments:
- images: bfloat16 [16384, 2048], P('img'), may hold values from -8 to 8
- references: bfloat16 [1024, 2048], P('ref'), may hold values from -1 to 1
- initial_contrast: float32 [16384], P('img'), may hold values from 0.25 to 1.75
Outputs:
- new_references: bfloat16 [1024, 2048], P('ref')
- contrast: float32 [16384], P('img')
- loglik: float32 [16384], P('img')
The draws below stay inside these ranges and needn't reach their ends.
All inputs are finite; a program needn't handle non-finite values.
Results may differ from the reference program's by a relative error of at most 0.0041.
Values may be sent and summed in bfloat16 or wider, within the bound.
A program may use at most 64 MiB of HBM per device.

```python
import math
import jax
import jax.numpy as jnp
from jax import lax

F = 2048
IMG_DEV = 1024
ITERS = 3
NIMG = 16384
NREF = 1024


def ref_table(key):
    subkey = jax.random.fold_in(key, 11)
    gaussian = jnp.clip(jax.random.normal(subkey, (NREF, F), jnp.float32), -4.0, 4.0)
    row_scale = 0.6 + 1.2 * jnp.arange(NREF, dtype=jnp.float32) / NREF
    return gaussian * row_scale[:, None] * F ** (-0.5)


def draw_references(key, part):
    return ref_table(key).astype(jnp.bfloat16)


def draw_images(key, part):
    subkey = jax.random.fold_in(key, 23)
    gaussian = jax.random.normal(subkey, (NIMG, F), jnp.float32)
    return jnp.clip(gaussian, -8.0, 8.0).astype(jnp.bfloat16)


def setup_inputs(seed: int = 0) -> dict:
    key_of = jax.random.split(jax.random.key(seed), 4)
    images = draw_images(jax.random.fold_in(key_of[3], 71), 0)
    references = draw_references(jax.random.fold_in(key_of[3], 71), 0)
    initial_contrast = jnp.clip(1.0 + 0.15 * jax.random.normal(key_of[2], (NIMG,), jnp.float32), 0.25, 1.75)
    return {"images": images, "references": references, "initial_contrast": initial_contrast}


sharpness = 2.0
prior_weight = 1.0
epsilon = 1e-06

def scores_of(cross_terms, ref_norms, contrast):
    contrast_col = contrast[:, None]
    return sharpness * (contrast_col * cross_terms - 0.5 * (contrast_col * contrast_col) * ref_norms[None, :])

def statistics(cross_terms, ref_norms, contrast):
    scored = scores_of(cross_terms, ref_norms, contrast)
    highest = lax.optimization_barrier(jnp.max(scored, axis=1))
    exponent = jnp.exp(scored - highest[:, None])
    summed = lax.optimization_barrier(jnp.sum(exponent, axis=1))
    weighted_cross = lax.optimization_barrier(jnp.sum(exponent * cross_terms, axis=1))
    weighted_norm = lax.optimization_barrier(jnp.sum(exponent * ref_norms[None, :], axis=1))
    return (highest, summed, weighted_cross, weighted_norm, exponent)

def normalize(sums):
    meansq = lax.optimization_barrier(jnp.mean(sums * sums, axis=1))
    return (sums * lax.rsqrt(meansq + epsilon)[:, None]).astype(jnp.bfloat16)

def reference(images, references, initial_contrast):
    ref_norms = lax.optimization_barrier(jnp.sum(jnp.square(references.astype(jnp.float32)), axis=1))
    image_blocks = images.reshape(NIMG // IMG_DEV, IMG_DEV, F)
    prior_blocks = initial_contrast.reshape(NIMG // IMG_DEV, IMG_DEV)

    def one_block(running, carried):
        image_block, prior = carried
        cross_terms = lax.dot_general(image_block, references, (((1,), (1,)), ((), ())), preferred_element_type=jnp.float32)
        contrast = prior
        for iteration in range(ITERS + 1):
            highest, summed, weighted_cross, weighted_norm, exponent = statistics(cross_terms, ref_norms, contrast)
            if iteration < ITERS:
                contrast = (weighted_cross / summed + prior_weight * prior) / (weighted_norm / summed + prior_weight)
        posterior = exponent / summed[:, None]
        weights = (posterior * contrast[:, None]).astype(jnp.bfloat16)
        running = running + lax.dot_general(weights, image_block, (((0,), (0,)), ((), ())), preferred_element_type=jnp.float32)
        return (running, contrast)
    sums, contrasts = lax.scan(one_block, jnp.zeros((NREF, F), jnp.float32), (image_blocks, prior_blocks))
    new_references = normalize(sums)
    new_norms = lax.optimization_barrier(jnp.sum(jnp.square(new_references.astype(jnp.float32)), axis=1)) / F

    def rescore(carried):
        image_block, contrast = carried
        new_cross = lax.dot_general(image_block, new_references, (((1,), (1,)), ((), ())), preferred_element_type=jnp.float32) * F ** (-0.5)
        highest, summed, weighted_cross, weighted_norm, exponent = statistics(new_cross, new_norms, contrast)
        return highest + jnp.log(summed) - math.log(NREF)
    loglik = lax.map(rescore, (image_blocks, contrasts))
    return (new_references, contrasts.reshape(NIMG), loglik.reshape(NIMG))
```

```python
import functools
import math

import jax
import jax.numpy as jnp
from jax import lax
from jax.experimental import pallas as pl
from jax.experimental.pallas import tpu as pltpu
from jax.sharding import PartitionSpec as P

ITERS = 3

sharpness = 2.0
prior_weight = 1.0
epsilon = 1e-06

MESH = pl.DeviceIdType.MESH
LANES = 256
QUADS = ((1, 0), (1, 1), (0, 1), (0, 0))
F32 = jnp.float32
BF16 = jnp.bfloat16


def kernel(
    nz, n_ref, im_hbm, ref_hbm, prior_ref, newref_hbm, contrast_ref, loglik_ref,
    im, refs, norms, cross, w, snd1, rcv1, acc, snd2, rcv2, snd3, rcv3, gath,
    stat_snd, stat_rcv, vecs, im_sem, ref_sem, out_sem, ssem, rsem,
):
    n, width = im.shape
    rows = refs.shape[0]
    rb = rows // (4 * nz)
    qr = nz * rb
    half = width // 2
    me = lax.axis_index("img")
    rme = lax.axis_index("ref")
    x, y, z = lax.rem(me, 2), lax.rem(me // 2, 2), me // 4
    counter = [0]

    def chip(dx, dy, dz):
        return lax.rem(z + dz, nz) * 4 + lax.rem(y + dy, 2) * 2 + lax.rem(x + dx, 2)

    def send(src, dst, dev):
        i = counter[0]
        counter[0] += 1
        copy = pltpu.make_async_remote_copy(
            src_ref=src, dst_ref=dst, send_sem=ssem.at[i], recv_sem=rsem.at[i],
            device_id=dev, device_id_type=MESH,
        )
        copy.start()
        sent.append(copy)
        return copy

    sent = []
    x_dev = {"img": chip(1, 0, 0)}
    y_dev = {"img": chip(0, 1, 0)}
    z_dev = [{"img": chip(0, 0, k)} for k in range(nz)]
    r_dev = [{"ref": lax.rem(rme + k, n_ref)} for k in range(n_ref)]

    ref_copies = []
    for q, (dx, dy) in enumerate(QUADS):
        for dz in range(nz):
            s = q * nz + dz
            copy = pltpu.make_async_copy(
                ref_hbm.at[pl.ds(chip(dx, dy, dz) * rb, rb)],
                refs.at[pl.ds(s * rb, rb)], ref_sem.at[s],
            )
            copy.start()
            ref_copies.append(copy)
    im_copies = []
    for b in range(n // LANES):
        part = pl.ds(b * LANES, LANES)
        copy = pltpu.make_async_copy(im_hbm.at[part], im.at[part], im_sem.at[b])
        copy.start()
        im_copies.append(copy)

    barrier = pltpu.get_barrier_semaphore()
    peers = [x_dev, y_dev] + z_dev[1:] + r_dev[1:]
    for dev in peers:
        pl.semaphore_signal(barrier, inc=1, device_id=dev, device_id_type=MESH)

    stat_snd[...] = jnp.zeros_like(stat_snd)
    vecs[0:1, :] = prior_ref[...]

    def square_sums(source, r0, count, scale):
        block = source[r0 : r0 + count, :].astype(F32)
        total = jnp.sum(block * block, axis=1, keepdims=True) * scale
        norms[r0 : r0 + count, :] = jnp.broadcast_to(total, (count, LANES))

    for s, copy in enumerate(ref_copies):
        copy.wait()
        square_sums(refs, s * rb, rb, 1.0)

    nt = (((1,), (1,)), ((), ()))
    nn = (((1,), (0,)), ((), ()))
    for copy in im_copies:
        copy.wait()

    def score_block(source, r0, count, scale):
        def body(b, carry):
            part = pl.ds(pl.multiple_of(b * LANES, LANES), LANES)
            out = lax.dot_general(
                source[r0 : r0 + count, :], im[part, :], nt, preferred_element_type=F32
            )
            cross[r0 : r0 + count, part] = out if scale is None else out * scale
            return carry

        lax.fori_loop(0, n // LANES, body, 0)

    score_block(refs, 0, rows, None)
    pl.semaphore_wait(barrier, len(peers))

    def scored(part):
        a = vecs[0:1, part]
        c = cross[:, part]
        return c, sharpness * (a * c - (0.5 * (a * a)) * norms[...])

    def statistics(it, full):
        def body(b, carry):
            part = pl.ds(pl.multiple_of(b * LANES, LANES), LANES)
            c, s = scored(part)
            top = jnp.max(s, axis=0, keepdims=True)
            e = jnp.exp(s - top)
            stat_snd[it, 0:1, part] = top
            stat_snd[it, 1:2, part] = jnp.sum(e, axis=0, keepdims=True)
            if full:
                stat_snd[it, 2:3, part] = jnp.sum(e * c, axis=0, keepdims=True)
                stat_snd[it, 3:4, part] = jnp.sum(e * norms[...], axis=0, keepdims=True)
            return carry

        lax.fori_loop(0, n // LANES, body, 0)
        copies = [
            send(stat_snd.at[it], stat_rcv.at[it * (n_ref - 1) + k - 1], r_dev[k])
            for k in range(1, n_ref)
        ]
        for copy in copies:
            copy.wait_recv()
        blocks = [stat_snd[it]] + [
            stat_rcv[it * (n_ref - 1) + k - 1] for k in range(1, n_ref)
        ]
        high = functools.reduce(jnp.maximum, [blk[0:1] for blk in blocks])
        scales = [jnp.exp(blk[0:1] - high) for blk in blocks]
        sums = [
            functools.reduce(jnp.add, [blk[j : j + 1] * sc for blk, sc in zip(blocks, scales)])
            for j in ((1, 2, 3) if full else (1,))
        ]
        return high, sums

    for it in range(ITERS):
        high, (total, along, weight) = statistics(it, True)
        vecs[0:1, :] = (along / total + prior_weight * prior_ref[...]) / (
            weight / total + prior_weight
        )
    high, (total,) = statistics(ITERS, False)
    vecs[1:2, :] = high
    vecs[2:3, :] = vecs[0:1, :] / total
    contrast_ref[...] = vecs[0:1, :]

    def weigh(b, carry):
        part = pl.ds(pl.multiple_of(b * LANES, LANES), LANES)
        _, s = scored(part)
        w[:, part] = (jnp.exp(s - vecs[1:2, part]) * vecs[2:3, part]).astype(BF16)
        return carry

    lax.fori_loop(0, n // LANES, weigh, 0)

    def weighted(r0s, c0, store):
        def body(b, carry):
            col = pl.multiple_of(b * LANES, LANES)
            lhs = [w[r0 : r0 + cnt, :] for r0, cnt in r0s]
            lhs = lhs[0] if len(lhs) == 1 else jnp.concatenate(lhs, axis=0)
            rhs = im[:, pl.ds(pl.multiple_of(c0 + col, LANES), LANES)]
            out = lax.dot_general(lhs, rhs, nn, preferred_element_type=F32)
            store(pl.ds(col, LANES), out[:qr], out[qr:])
            return carry

        lax.fori_loop(0, half // LANES, body, 0)

    def to_send(stream, first_is_far):
        def store(cols, lo, hi):
            far, near = (lo, hi) if first_is_far else (hi, lo)
            snd1[stream * 2, :, cols] = far.astype(BF16)
            snd1[stream * 2 + 1, :, cols] = near.astype(BF16)

        return store

    def to_keep(stream):
        def store(cols, lo, hi):
            acc[stream * 2, :, cols] = lo
            acc[stream * 2 + 1, :, cols] = hi

        return store

    weighted([(0, 2 * qr)], 0, to_send(0, False))
    step1 = [[send(snd1.at[j], rcv1.at[j], x_dev) for j in (0, 1)]]
    weighted([(qr, 2 * qr)], half, to_send(1, True))
    step1.append([send(snd1.at[j], rcv1.at[j], y_dev) for j in (2, 3)])
    weighted([(2 * qr, 2 * qr)], 0, to_keep(0))
    weighted([(0, qr), (3 * qr, qr)], half, to_keep(1))

    z_order = sorted(range(1, nz), key=lambda k: (min(k, nz - k), k))
    far_order = z_order[::-1]
    step2 = [{}, {}]
    for s, dev in ((0, y_dev), (1, x_dev)):
        step1[s][0].wait_recv()
        snd2[s] = (acc[s * 2] + rcv1[s * 2].astype(F32)).astype(BF16)
        for dz in far_order + [0]:
            part = pl.ds(dz * rb, rb)
            step2[s][dz] = send(snd2.at[s, part], rcv2.at[s, part], dev)
    for s in (0, 1):
        step1[s][1].wait_recv()
        acc[s * 2 + 1] = acc[s * 2 + 1] + rcv1[s * 2 + 1].astype(F32)
    step3 = []
    for dz in far_order:
        r0 = dz * rb
        for s in (0, 1):
            step2[s][dz].wait_recv()
            snd3[s, dz - 1] = (
                acc[s * 2 + 1, r0 : r0 + rb, :] + rcv2[s, r0 : r0 + rb, :].astype(F32)
            ).astype(BF16)
            step3.append((s, dz, send(snd3.at[s, dz - 1], rcv3.at[s, dz - 1], z_dev[dz])))
    for s in (0, 1):
        step2[s][0].wait_recv()
        acc[s * 2 + 1, 0:rb, :] = acc[s * 2 + 1, 0:rb, :] + rcv2[s, 0:rb, :].astype(F32)
    for s, dz, copy in step3:
        copy.wait_recv()
        acc[s * 2 + 1, 0:rb, :] = acc[s * 2 + 1, 0:rb, :] + rcv3[s, dz - 1].astype(F32)

    left, right = acc[1, 0:rb, :], acc[3, 0:rb, :]
    square = jnp.sum(left * left, axis=1, keepdims=True) + jnp.sum(
        right * right, axis=1, keepdims=True
    )
    factor = lax.rsqrt(square / width + epsilon)
    own = 3 * qr
    gath[own : own + rb, 0:half] = (left * factor).astype(BF16)
    gath[own : own + rb, half:width] = (right * factor).astype(BF16)

    def piece(q, dz, s):
        return gath.at[pl.ds(q * qr + dz * rb, rb), pl.ds(s * half, half)]

    def slot(q, dz):
        return gath.at[pl.ds(q * qr + dz * rb, rb)]

    along_z = {}
    for k in far_order:
        along_z[nz - k] = send(slot(3, 0), slot(3, nz - k), z_dev[k])
    into_x, into_y, last = {}, {}, []

    def spread(dz):
        into_y[dz] = [send(piece(3, dz, 0), piece(2, dz, 0), y_dev)]
        into_x[dz] = [send(piece(3, dz, 1), piece(0, dz, 1), x_dev)]
        into_y[dz].append(send(piece(3, dz, 1), piece(2, dz, 1), y_dev))
        into_x[dz].append(send(piece(3, dz, 0), piece(0, dz, 0), x_dev))

    def forward(dz):
        into_y[dz][0].wait_recv()
        last.append(send(piece(2, dz, 0), piece(1, dz, 0), x_dev))
        into_x[dz][0].wait_recv()
        last.append(send(piece(0, dz, 1), piece(1, dz, 1), y_dev))

    outs = []

    def rescore(q):
        dx, dy = QUADS[q]
        for dz in range(nz):
            copy = pltpu.make_async_copy(
                slot(q, dz), newref_hbm.at[pl.ds(chip(dx, dy, dz) * rb, rb)],
                out_sem.at[q * nz + dz],
            )
            copy.start()
            outs.append(copy)
        score_block(gath, q * qr, qr, width ** (-0.5))
        square_sums(gath, q * qr, qr, 1.0 / width)

    spread(0)
    before = 0
    for dz in z_order:
        along_z[dz].wait_recv()
        spread(dz)
        if dz == z_order[-1]:
            forward(before)
            rescore(3)
            forward(dz)
        else:
            forward(before)
        before = dz
    if not z_order:
        rescore(3)
        forward(0)
    for q, into in ((0, into_x), (2, into_y)):
        for dz in range(nz):
            j = 1 if q == 0 else 1
            into[dz][j].wait_recv()
        rescore(q)
    for copy in last:
        copy.wait_recv()
    rescore(1)

    high, (total,) = statistics(ITERS + 1, False)
    loglik_ref[...] = high + jnp.log(total) - math.log(rows * n_ref)
    for copy in outs:
        copy.wait()
    for copy in sent:
        copy.wait_send()


def per_device(nz, n_ref, images, references, initial_contrast):
    n, width = images.shape
    rows = references.shape[0]
    rb = rows // (4 * nz)
    qr, half = nz * rb, width // 2
    steps = ITERS + 2
    copies = steps * (n_ref - 1) + 4 + 2 * nz + 2 * (nz - 1) + (nz - 1) + 6 * nz
    peers = max(n_ref - 1, 1)
    flops = 6 * n * width * rows
    new_references, contrast, loglik = pl.pallas_call(
        functools.partial(kernel, nz, n_ref),
        out_shape=(
            jax.ShapeDtypeStruct((rows, width), BF16),
            jax.ShapeDtypeStruct((1, n), F32),
            jax.ShapeDtypeStruct((1, n), F32),
        ),
        in_specs=[
            pl.BlockSpec(memory_space=pl.ANY),
            pl.BlockSpec(memory_space=pl.ANY),
            pl.BlockSpec(memory_space=pltpu.VMEM),
        ],
        out_specs=(
            pl.BlockSpec(memory_space=pl.ANY),
            pl.BlockSpec(memory_space=pltpu.VMEM),
            pl.BlockSpec(memory_space=pltpu.VMEM),
        ),
        scratch_shapes=[
            pltpu.VMEM((n, width), BF16),
            pltpu.VMEM((rows, width), BF16),
            pltpu.VMEM((rows, LANES), F32),
            pltpu.VMEM((rows, n), F32),
            pltpu.VMEM((rows, n), BF16),
            pltpu.VMEM((4, qr, half), BF16),
            pltpu.VMEM((4, qr, half), BF16),
            pltpu.VMEM((4, qr, half), F32),
            pltpu.VMEM((2, qr, half), BF16),
            pltpu.VMEM((2, qr, half), BF16),
            pltpu.VMEM((2, max(nz - 1, 1), rb, half), BF16),
            pltpu.VMEM((2, max(nz - 1, 1), rb, half), BF16),
            pltpu.VMEM((rows, width), BF16),
            pltpu.VMEM((steps, 8, n), F32),
            pltpu.VMEM((steps * peers, 8, n), F32),
            pltpu.VMEM((8, n), F32),
            pltpu.SemaphoreType.DMA((n // LANES,)),
            pltpu.SemaphoreType.DMA((4 * nz,)),
            pltpu.SemaphoreType.DMA((4 * nz,)),
            pltpu.SemaphoreType.DMA((copies,)),
            pltpu.SemaphoreType.DMA((copies,)),
        ],
        compiler_params=pltpu.CompilerParams(
            collective_id=0, has_side_effects=True, vmem_limit_bytes=56 * 1024 * 1024
        ),
        cost_estimate=pl.CostEstimate(
            flops=flops, bytes_accessed=2 * n * width, transcendentals=0
        ),
    )(images, references, initial_contrast[None, :])
    return (new_references, contrast[0], loglik[0])


def solution(mesh):
    n_img, n_ref = mesh.shape["img"], mesh.shape["ref"]
    placed = (P("img", None), P("ref", None), P("img"))
    return jax.shard_map(
        functools.partial(per_device, n_img // 4, n_ref),
        mesh=mesh,
        in_specs=placed,
        out_specs=(P("ref", None), P("img"), P("img")),
        check_vma=False,
    )
```

```python
import functools
import math

import jax
import jax.numpy as jnp
from jax import lax
from jax.experimental import pallas as pl
from jax.experimental.pallas import tpu as pltpu
from jax.sharding import PartitionSpec as P

ITERS = 3

sharpness = 2.0
prior_weight = 1.0
epsilon = 1e-06

MESH = pl.DeviceIdType.MESH
LANES = 256
QUADS = ((1, 0), (1, 1), (0, 1), (0, 0))
F32 = jnp.float32
BF16 = jnp.bfloat16


def kernel(
    nz, n_ref, im_hbm, ref_hbm, prior_ref, newref_hbm, contrast_ref, loglik_ref,
    im, refs, norms, cross, w, snd1, rcv1, acc, snd2, rcv2, snd3, rcv3, gath,
    stat_snd, stat_rcv, vecs, im_sem, ref_sem, out_sem, ssem, rsem,
):
    n, width = im.shape
    rows = refs.shape[0]
    rb = rows // (4 * nz)
    qr = nz * rb
    half = width // 2
    me = lax.axis_index("img")
    rme = lax.axis_index("ref")
    x, y, z = lax.rem(me, 2), lax.rem(me // 2, 2), me // 4
    counter = [0]

    def chip(dx, dy, dz):
        zz, bit = z, 1
        while bit < nz:
            if dz & bit:
                zz = zz + bit - 2 * bit * lax.rem(z // bit, 2)
            bit *= 2
        return zz * 4 + lax.rem(y + dy, 2) * 2 + lax.rem(x + dx, 2)

    def send(src, dst, dev):
        i = counter[0]
        counter[0] += 1
        copy = pltpu.make_async_remote_copy(
            src_ref=src, dst_ref=dst, send_sem=ssem.at[i], recv_sem=rsem.at[i],
            device_id=dev, device_id_type=MESH,
        )
        copy.start()
        sent.append(copy)
        return copy

    sent = []
    x_dev = {"img": chip(1, 0, 0)}
    y_dev = {"img": chip(0, 1, 0)}
    z_dev = [{"img": chip(0, 0, k)} for k in range(nz)]
    r_dev = [{"ref": lax.rem(rme + k, n_ref)} for k in range(n_ref)]

    ref_copies = []
    for q, (dx, dy) in enumerate(QUADS):
        for dz in range(nz):
            s = q * nz + dz
            copy = pltpu.make_async_copy(
                ref_hbm.at[pl.ds(chip(dx, dy, dz) * rb, rb)],
                refs.at[pl.ds(s * rb, rb)], ref_sem.at[s],
            )
            copy.start()
            ref_copies.append(copy)
    im_copies = []
    for b in range(n // LANES):
        part = pl.ds(b * LANES, LANES)
        copy = pltpu.make_async_copy(im_hbm.at[part], im.at[part], im_sem.at[b])
        copy.start()
        im_copies.append(copy)

    barrier = pltpu.get_barrier_semaphore()
    peers = [x_dev, y_dev] + [z_dev[k] for k in range(1, nz) if k & (k - 1) == 0] + r_dev[1:]
    for dev in peers:
        pl.semaphore_signal(barrier, inc=1, device_id=dev, device_id_type=MESH)

    stat_snd[...] = jnp.zeros_like(stat_snd)
    vecs[0:1, :] = prior_ref[...]

    def square_sums(source, r0, count, scale):
        block = source[r0 : r0 + count, :].astype(F32)
        total = jnp.sum(block * block, axis=1, keepdims=True) * scale
        norms[r0 : r0 + count, :] = jnp.broadcast_to(total, (count, LANES))

    for s, copy in enumerate(ref_copies):
        copy.wait()
        square_sums(refs, s * rb, rb, 1.0)

    nt = (((1,), (1,)), ((), ()))
    nn = (((1,), (0,)), ((), ()))
    for copy in im_copies:
        copy.wait()

    def score_block(source, r0, count, scale):
        def body(b, carry):
            part = pl.ds(pl.multiple_of(b * LANES, LANES), LANES)
            out = lax.dot_general(
                source[r0 : r0 + count, :], im[part, :], nt, preferred_element_type=F32
            )
            cross[r0 : r0 + count, part] = out if scale is None else out * scale
            return carry

        lax.fori_loop(0, n // LANES, body, 0)

    score_block(refs, 0, rows, None)
    pl.semaphore_wait(barrier, len(peers))

    def scored(part):
        a = vecs[0:1, part]
        c = cross[:, part]
        return c, sharpness * (a * c - (0.5 * (a * a)) * norms[...])

    def statistics(it, full):
        def body(b, carry):
            part = pl.ds(pl.multiple_of(b * LANES, LANES), LANES)
            c, s = scored(part)
            top = jnp.max(s, axis=0, keepdims=True)
            e = jnp.exp(s - top)
            stat_snd[it, 0:1, part] = top
            stat_snd[it, 1:2, part] = jnp.sum(e, axis=0, keepdims=True)
            if full:
                stat_snd[it, 2:3, part] = jnp.sum(e * c, axis=0, keepdims=True)
                stat_snd[it, 3:4, part] = jnp.sum(e * norms[...], axis=0, keepdims=True)
            return carry

        lax.fori_loop(0, n // LANES, body, 0)
        copies = [
            send(stat_snd.at[it], stat_rcv.at[it * (n_ref - 1) + k - 1], r_dev[k])
            for k in range(1, n_ref)
        ]
        for copy in copies:
            copy.wait_recv()
        blocks = [stat_snd[it]] + [
            stat_rcv[it * (n_ref - 1) + k - 1] for k in range(1, n_ref)
        ]
        high = functools.reduce(jnp.maximum, [blk[0:1] for blk in blocks])
        scales = [jnp.exp(blk[0:1] - high) for blk in blocks]
        sums = [
            functools.reduce(jnp.add, [blk[j : j + 1] * sc for blk, sc in zip(blocks, scales)])
            for j in ((1, 2, 3) if full else (1,))
        ]
        return high, sums

    for it in range(ITERS):
        high, (total, along, weight) = statistics(it, True)
        vecs[0:1, :] = (along / total + prior_weight * prior_ref[...]) / (
            weight / total + prior_weight
        )
    high, (total,) = statistics(ITERS, False)
    vecs[1:2, :] = high
    vecs[2:3, :] = vecs[0:1, :] / total
    contrast_ref[...] = vecs[0:1, :]

    def weigh(b, carry):
        part = pl.ds(pl.multiple_of(b * LANES, LANES), LANES)
        _, s = scored(part)
        w[:, part] = (jnp.exp(s - vecs[1:2, part]) * vecs[2:3, part]).astype(BF16)
        return carry

    lax.fori_loop(0, n // LANES, weigh, 0)

    def weighted(r0s, c0, store):
        def body(b, carry):
            col = pl.multiple_of(b * LANES, LANES)
            lhs = [w[r0 : r0 + cnt, :] for r0, cnt in r0s]
            lhs = lhs[0] if len(lhs) == 1 else jnp.concatenate(lhs, axis=0)
            rhs = im[:, pl.ds(pl.multiple_of(c0 + col, LANES), LANES)]
            out = lax.dot_general(lhs, rhs, nn, preferred_element_type=F32)
            store(pl.ds(col, LANES), out[:qr], out[qr:])
            return carry

        lax.fori_loop(0, half // LANES, body, 0)

    def to_send(stream, first_is_far):
        def store(cols, lo, hi):
            far, near = (lo, hi) if first_is_far else (hi, lo)
            snd1[stream * 2, :, cols] = far.astype(BF16)
            snd1[stream * 2 + 1, :, cols] = near.astype(BF16)

        return store

    def to_keep(stream):
        def store(cols, lo, hi):
            acc[stream * 2, :, cols] = lo
            acc[stream * 2 + 1, :, cols] = hi

        return store

    low = [dz & -dz for dz in range(nz)]
    order = sorted(range(1, nz), key=lambda k: (low[k], -k)) + [0]
    early = [dz for dz in order if low[dz] == 1] or order
    late = [dz for dz in order if dz not in early]
    hop_dev = (x_dev, y_dev)
    step1 = {}

    def send1(s, j, dzs):
        for dz in dzs:
            part = pl.ds(dz * rb, rb)
            step1[s, j, dz] = send(
                snd1.at[s * 2 + j, part], rcv1.at[s * 2 + j, part], hop_dev[s]
            )

    weighted([(0, 2 * qr)], 0, to_send(0, False))
    send1(0, 0, early)
    send1(0, 1, early)
    weighted([(qr, 2 * qr)], half, to_send(1, True))
    send1(1, 0, early)
    send1(1, 1, early)
    weighted([(2 * qr, 2 * qr)], 0, to_keep(0))
    weighted([(0, qr), (3 * qr, qr)], half, to_keep(1))

    step2 = {}

    def send2(dzs):
        for dz in dzs:
            r0 = dz * rb
            part = pl.ds(r0, rb)
            for s in (1, 0):
                step1[s, 0, dz].wait_recv()
                snd2[s, r0 : r0 + rb, :] = (
                    acc[s * 2, r0 : r0 + rb, :] + rcv1[s * 2, r0 : r0 + rb, :].astype(F32)
                ).astype(BF16)
                step2[s, dz] = send(snd2.at[s, part], rcv2.at[s, part], hop_dev[1 - s])

    def gained(s, dz):
        step1[s, 1, dz].wait_recv()
        step2[s, dz].wait_recv()
        r0 = dz * rb
        return (
            acc[s * 2 + 1, r0 : r0 + rb, :]
            + rcv1[s * 2 + 1, r0 : r0 + rb, :].astype(F32)
            + rcv2[s, r0 : r0 + rb, :].astype(F32)
        )

    send2(early)
    for j in (0, 1):
        for s in (0, 1):
            send1(s, j, late)
    send2(late)

    step3 = {}

    def complete(s, dz):
        total = gained(s, dz)
        for k in range(nz):
            if low[k] and k - low[k] == dz and (dz == 0 or low[k] < low[dz]):
                step3[s, k].wait_recv()
                total = total + rcv3[s, k - 1].astype(F32)
        return total

    for dz in order[:-1]:
        for s in (0, 1):
            snd3[s, dz - 1] = complete(s, dz).astype(BF16)
            step3[s, dz] = send(snd3.at[s, dz - 1], rcv3.at[s, dz - 1], z_dev[low[dz]])
    for s in (0, 1):
        acc[s * 2 + 1, 0:rb, :] = complete(s, 0)

    left, right = acc[1, 0:rb, :], acc[3, 0:rb, :]
    square = jnp.sum(left * left, axis=1, keepdims=True) + jnp.sum(
        right * right, axis=1, keepdims=True
    )
    factor = lax.rsqrt(square / width + epsilon)
    own = 3 * qr
    gath[own : own + rb, 0:half] = (left * factor).astype(BF16)
    gath[own : own + rb, half:width] = (right * factor).astype(BF16)

    def piece(q, dz, s):
        return gath.at[pl.ds(q * qr + dz * rb, rb), pl.ds(s * half, half)]

    def slot(q, dz):
        return gath.at[pl.ds(q * qr + dz * rb, rb)]

    along_z = {}

    def double(dz, bits):
        for bit in bits:
            along_z[dz + bit] = send(slot(3, dz), slot(3, dz + bit), z_dev[bit])

    bits = [1 << j for j in range(nz.bit_length() - 1)]
    into_x, into_y, last = {}, {}, []

    def spread(dz):
        into_y[dz] = [send(piece(3, dz, 0), piece(2, dz, 0), y_dev)]
        into_x[dz] = [send(piece(3, dz, 1), piece(0, dz, 1), x_dev)]
        into_y[dz].append(send(piece(3, dz, 1), piece(2, dz, 1), y_dev))
        into_x[dz].append(send(piece(3, dz, 0), piece(0, dz, 0), x_dev))

    def forward(dz):
        into_y[dz][0].wait_recv()
        last.append(send(piece(2, dz, 0), piece(1, dz, 0), x_dev))
        into_x[dz][0].wait_recv()
        last.append(send(piece(0, dz, 1), piece(1, dz, 1), y_dev))

    outs = []

    def rescore(q0, count):
        for q in range(q0, q0 + count):
            dx, dy = QUADS[q]
            for dz in range(nz):
                copy = pltpu.make_async_copy(
                    slot(q, dz), newref_hbm.at[pl.ds(chip(dx, dy, dz) * rb, rb)],
                    out_sem.at[q * nz + dz],
                )
                copy.start()
                outs.append(copy)
        score_block(gath, q0 * qr, count * qr, width ** (-0.5))
        square_sums(gath, q0 * qr, count * qr, 1.0 / width)

    double(0, bits)
    spread(0)
    arrivals = sorted(range(1, nz), key=lambda k: (k.bit_count(), k))
    before = 0
    for dz in arrivals:
        along_z[dz].wait_recv()
        double(dz, [bit for bit in bits if bit < low[dz]])
        spread(dz)
        forward(before)
        before = dz
    forward(before)
    for dz in range(nz):
        into_y[dz][1].wait_recv()
    rescore(2, 2)
    for dz in range(nz):
        into_x[dz][1].wait_recv()
    for copy in last:
        copy.wait_recv()
    rescore(0, 2)

    high, (total,) = statistics(ITERS + 1, False)
    loglik_ref[...] = high + jnp.log(total) - math.log(rows * n_ref)
    for copy in outs:
        copy.wait()
    for copy in sent:
        copy.wait_send()


def per_device(nz, n_ref, images, references, initial_contrast):
    n, width = images.shape
    rows = references.shape[0]
    rb = rows // (4 * nz)
    qr, half = nz * rb, width // 2
    steps = ITERS + 2
    copies = steps * (n_ref - 1) + 6 * nz + 2 * (nz - 1) + (nz - 1) + 6 * nz
    peers = max(n_ref - 1, 1)
    flops = 6 * n * width * rows
    new_references, contrast, loglik = pl.pallas_call(
        functools.partial(kernel, nz, n_ref),
        out_shape=(
            jax.ShapeDtypeStruct((rows, width), BF16),
            jax.ShapeDtypeStruct((1, n), F32),
            jax.ShapeDtypeStruct((1, n), F32),
        ),
        in_specs=[
            pl.BlockSpec(memory_space=pl.ANY),
            pl.BlockSpec(memory_space=pl.ANY),
            pl.BlockSpec(memory_space=pltpu.VMEM),
        ],
        out_specs=(
            pl.BlockSpec(memory_space=pl.ANY),
            pl.BlockSpec(memory_space=pltpu.VMEM),
            pl.BlockSpec(memory_space=pltpu.VMEM),
        ),
        scratch_shapes=[
            pltpu.VMEM((n, width), BF16),
            pltpu.VMEM((rows, width), BF16),
            pltpu.VMEM((rows, LANES), F32),
            pltpu.VMEM((rows, n), F32),
            pltpu.VMEM((rows, n), BF16),
            pltpu.VMEM((4, qr, half), BF16),
            pltpu.VMEM((4, qr, half), BF16),
            pltpu.VMEM((4, qr, half), F32),
            pltpu.VMEM((2, qr, half), BF16),
            pltpu.VMEM((2, qr, half), BF16),
            pltpu.VMEM((2, max(nz - 1, 1), rb, half), BF16),
            pltpu.VMEM((2, max(nz - 1, 1), rb, half), BF16),
            pltpu.VMEM((rows, width), BF16),
            pltpu.VMEM((steps, 8, n), F32),
            pltpu.VMEM((steps * peers, 8, n), F32),
            pltpu.VMEM((8, n), F32),
            pltpu.SemaphoreType.DMA((n // LANES,)),
            pltpu.SemaphoreType.DMA((4 * nz,)),
            pltpu.SemaphoreType.DMA((4 * nz,)),
            pltpu.SemaphoreType.DMA((copies,)),
            pltpu.SemaphoreType.DMA((copies,)),
        ],
        compiler_params=pltpu.CompilerParams(
            collective_id=0, has_side_effects=True, vmem_limit_bytes=56 * 1024 * 1024
        ),
        cost_estimate=pl.CostEstimate(
            flops=flops, bytes_accessed=2 * n * width, transcendentals=0
        ),
    )(images, references, initial_contrast[None, :])
    return (new_references, contrast[0], loglik[0])


def solution(mesh):
    n_img, n_ref = mesh.shape["img"], mesh.shape["ref"]
    placed = (P("img", None), P("ref", None), P("img"))
    return jax.shard_map(
        functools.partial(per_device, n_img // 4, n_ref),
        mesh=mesh,
        in_specs=placed,
        out_specs=(P("ref", None), P("img"), P("img")),
        check_vma=False,
    )
```

```python
import functools
import math

import jax
import jax.numpy as jnp
from jax import lax
from jax.experimental import pallas as pl
from jax.experimental.pallas import tpu as pltpu
from jax.sharding import PartitionSpec as P

ITERS = 3

sharpness = 2.0
prior_weight = 1.0
epsilon = 1e-06

MESH = pl.DeviceIdType.MESH
LANES = 256
QUADS = ((1, 0), (1, 1), (0, 1), (0, 0))
F32 = jnp.float32
BF16 = jnp.bfloat16


def kernel(
    nz, n_ref, im_hbm, ref_hbm, prior_ref, newref_hbm, contrast_ref, loglik_ref,
    im, refs, norms, cross, w, snd1, rcv1, acc, snd2, rcv2, snd3, rcv3, gath,
    stat_snd, stat_rcv, vecs, im_sem, ref_sem, out_sem, ssem, rsem,
):
    n, width = im.shape
    rows = refs.shape[0]
    rb = rows // (4 * nz)
    qr = nz * rb
    half = width // 2
    me = lax.axis_index("img")
    rme = lax.axis_index("ref")
    x, y, z = lax.rem(me, 2), lax.rem(me // 2, 2), me // 4
    counter = [0]

    def chip(dx, dy, dz):
        zz, bit = z, 1
        while bit < nz:
            if dz & bit:
                zz = zz + bit - 2 * bit * lax.rem(z // bit, 2)
            bit *= 2
        return zz * 4 + lax.rem(y + dy, 2) * 2 + lax.rem(x + dx, 2)

    def send(src, dst, dev):
        i = counter[0]
        counter[0] += 1
        copy = pltpu.make_async_remote_copy(
            src_ref=src, dst_ref=dst, send_sem=ssem.at[i], recv_sem=rsem.at[i],
            device_id=dev, device_id_type=MESH,
        )
        copy.start()
        sent.append(copy)
        return copy

    sent = []
    x_dev = {"img": chip(1, 0, 0)}
    y_dev = {"img": chip(0, 1, 0)}
    z_dev = [{"img": chip(0, 0, k)} for k in range(nz)]
    r_dev = [{"ref": lax.rem(rme + k, n_ref)} for k in range(n_ref)]

    ref_copies = []
    for q, (dx, dy) in enumerate(QUADS):
        for dz in range(nz):
            s = q * nz + dz
            copy = pltpu.make_async_copy(
                ref_hbm.at[pl.ds(chip(dx, dy, dz) * rb, rb)],
                refs.at[pl.ds(s * rb, rb)], ref_sem.at[s],
            )
            copy.start()
            ref_copies.append(copy)
    im_copies = []
    for b in range(n // LANES):
        part = pl.ds(b * LANES, LANES)
        copy = pltpu.make_async_copy(im_hbm.at[part], im.at[part], im_sem.at[b])
        copy.start()
        im_copies.append(copy)

    barrier = pltpu.get_barrier_semaphore()
    peers = [x_dev, y_dev] + [z_dev[k] for k in range(1, nz) if k & (k - 1) == 0] + r_dev[1:]
    for dev in peers:
        pl.semaphore_signal(barrier, inc=1, device_id=dev, device_id_type=MESH)

    stat_snd[...] = jnp.zeros_like(stat_snd)
    vecs[0:1, :] = prior_ref[...]

    def square_sums(source, r0, count, scale):
        block = source[r0 : r0 + count, :].astype(F32)
        total = jnp.sum(block * block, axis=1, keepdims=True) * scale
        norms[r0 : r0 + count, :] = jnp.broadcast_to(total, (count, LANES))

    for s, copy in enumerate(ref_copies):
        copy.wait()
        square_sums(refs, s * rb, rb, 1.0)

    nt = (((1,), (1,)), ((), ()))
    nn = (((1,), (0,)), ((), ()))
    for copy in im_copies:
        copy.wait()

    def score_block(source, r0, count, scale):
        def body(b, carry):
            part = pl.ds(pl.multiple_of(b * LANES, LANES), LANES)
            out = lax.dot_general(
                source[r0 : r0 + count, :], im[part, :], nt, preferred_element_type=F32
            )
            cross[r0 : r0 + count, part] = out if scale is None else out * scale
            return carry

        lax.fori_loop(0, n // LANES, body, 0)

    score_block(refs, 0, rows, None)
    pl.semaphore_wait(barrier, len(peers))

    def scored(part):
        a = vecs[0:1, part]
        c = cross[:, part]
        return c, (sharpness * a) * c - ((0.5 * sharpness) * (a * a)) * norms[...]

    def statistics(it, full):
        def body(b, carry):
            part = pl.ds(pl.multiple_of(b * LANES, LANES), LANES)
            c, s = scored(part)
            top = jnp.max(s, axis=0, keepdims=True)
            e = jnp.exp(s - top)
            stat_snd[it, 0:1, part] = top
            stat_snd[it, 1:2, part] = jnp.sum(e, axis=0, keepdims=True)
            if full:
                stat_snd[it, 2:3, part] = jnp.sum(e * c, axis=0, keepdims=True)
                stat_snd[it, 3:4, part] = jnp.sum(e * norms[...], axis=0, keepdims=True)
            return carry

        lax.fori_loop(0, n // LANES, body, 0)
        copies = [
            send(stat_snd.at[it], stat_rcv.at[it * (n_ref - 1) + k - 1], r_dev[k])
            for k in range(1, n_ref)
        ]
        for copy in copies:
            copy.wait_recv()
        blocks = [stat_snd[it]] + [
            stat_rcv[it * (n_ref - 1) + k - 1] for k in range(1, n_ref)
        ]
        high = functools.reduce(jnp.maximum, [blk[0:1] for blk in blocks])
        scales = [jnp.exp(blk[0:1] - high) for blk in blocks]
        sums = [
            functools.reduce(jnp.add, [blk[j : j + 1] * sc for blk, sc in zip(blocks, scales)])
            for j in ((1, 2, 3) if full else (1,))
        ]
        return high, sums

    for it in range(ITERS):
        high, (total, along, weight) = statistics(it, True)
        vecs[0:1, :] = (along / total + prior_weight * prior_ref[...]) / (
            weight / total + prior_weight
        )
    high, (total,) = statistics(ITERS, False)
    vecs[1:2, :] = high
    vecs[2:3, :] = vecs[0:1, :] / total
    contrast_ref[...] = vecs[0:1, :]

    def weigh(b, carry):
        part = pl.ds(pl.multiple_of(b * LANES, LANES), LANES)
        _, s = scored(part)
        w[:, part] = (jnp.exp(s - vecs[1:2, part]) * vecs[2:3, part]).astype(BF16)
        return carry

    lax.fori_loop(0, n // LANES, weigh, 0)

    def weighted(r0s, c0, store):
        def body(b, carry):
            col = pl.multiple_of(b * LANES, LANES)
            lhs = [w[r0 : r0 + cnt, :] for r0, cnt in r0s]
            lhs = lhs[0] if len(lhs) == 1 else jnp.concatenate(lhs, axis=0)
            rhs = im[:, pl.ds(pl.multiple_of(c0 + col, LANES), LANES)]
            out = lax.dot_general(lhs, rhs, nn, preferred_element_type=F32)
            store(pl.ds(col, LANES), out[:qr], out[qr:])
            return carry

        lax.fori_loop(0, half // LANES, body, 0)

    def to_send(stream, first_is_far):
        def store(cols, lo, hi):
            far, near = (lo, hi) if first_is_far else (hi, lo)
            snd1[stream * 2, :, cols] = far.astype(BF16)
            snd1[stream * 2 + 1, :, cols] = near.astype(BF16)

        return store

    def to_keep(stream):
        def store(cols, lo, hi):
            acc[stream * 2, :, cols] = lo
            acc[stream * 2 + 1, :, cols] = hi

        return store

    low = [dz & -dz for dz in range(nz)]
    order = sorted(range(1, nz), key=lambda k: (low[k], -k)) + [0]
    early = [dz for dz in order if low[dz] == 1] or order
    late = [dz for dz in order if dz not in early]
    hop_dev = (x_dev, y_dev)
    step1 = {}

    def send1(s, j, dzs):
        for dz in dzs:
            part = pl.ds(dz * rb, rb)
            step1[s, j, dz] = send(
                snd1.at[s * 2 + j, part], rcv1.at[s * 2 + j, part], hop_dev[s]
            )

    weighted([(0, 2 * qr)], 0, to_send(0, False))
    send1(0, 0, early)
    send1(0, 1, early)
    weighted([(qr, 2 * qr)], half, to_send(1, True))
    send1(1, 0, early)
    send1(1, 1, early)
    weighted([(2 * qr, 2 * qr)], 0, to_keep(0))
    weighted([(0, qr), (3 * qr, qr)], half, to_keep(1))

    step2 = {}

    def send2(dzs):
        for dz in dzs:
            r0 = dz * rb
            part = pl.ds(r0, rb)
            for s in (1, 0):
                step1[s, 0, dz].wait_recv()
                snd2[s, r0 : r0 + rb, :] = (
                    acc[s * 2, r0 : r0 + rb, :] + rcv1[s * 2, r0 : r0 + rb, :].astype(F32)
                ).astype(BF16)
                step2[s, dz] = send(snd2.at[s, part], rcv2.at[s, part], hop_dev[1 - s])

    def gained(s, dz):
        step1[s, 1, dz].wait_recv()
        step2[s, dz].wait_recv()
        r0 = dz * rb
        return (
            acc[s * 2 + 1, r0 : r0 + rb, :]
            + rcv1[s * 2 + 1, r0 : r0 + rb, :].astype(F32)
            + rcv2[s, r0 : r0 + rb, :].astype(F32)
        )

    step3 = {}

    def complete(s, dz):
        total = gained(s, dz)
        for k in range(nz):
            if low[k] and k - low[k] == dz and (dz == 0 or low[k] < low[dz]):
                step3[s, k].wait_recv()
                total = total + rcv3[s, k - 1].astype(F32)
        return total

    def send3(dzs):
        for dz in dzs:
            for s in (0, 1):
                snd3[s, dz - 1] = complete(s, dz).astype(BF16)
                step3[s, dz] = send(
                    snd3.at[s, dz - 1], rcv3.at[s, dz - 1], z_dev[low[dz]]
                )

    send2(early)
    for j in (0, 1):
        for s in (0, 1):
            send1(s, j, late)
    if late:
        send3(early)
    send2(late)
    send3([dz for dz in late if dz])
    for s in (0, 1):
        acc[s * 2 + 1, 0:rb, :] = complete(s, 0)

    left, right = acc[1, 0:rb, :], acc[3, 0:rb, :]
    square = jnp.sum(left * left, axis=1, keepdims=True) + jnp.sum(
        right * right, axis=1, keepdims=True
    )
    factor = lax.rsqrt(square / width + epsilon)
    own = 3 * qr
    gath[own : own + rb, 0:half] = (left * factor).astype(BF16)
    gath[own : own + rb, half:width] = (right * factor).astype(BF16)

    def piece(q, dz, s):
        return gath.at[pl.ds(q * qr + dz * rb, rb), pl.ds(s * half, half)]

    def slot(q, dz):
        return gath.at[pl.ds(q * qr + dz * rb, rb)]

    along_z = {}

    def double(dz, bits):
        for bit in bits:
            along_z[dz + bit] = send(slot(3, dz), slot(3, dz + bit), z_dev[bit])

    bits = [1 << j for j in range(nz.bit_length() - 1)]
    into_x, into_y, last = {}, {}, []

    def spread(dz):
        into_y[dz] = [send(piece(3, dz, 0), piece(2, dz, 0), y_dev)]
        into_x[dz] = [send(piece(3, dz, 1), piece(0, dz, 1), x_dev)]
        into_y[dz].append(send(piece(3, dz, 1), piece(2, dz, 1), y_dev))
        into_x[dz].append(send(piece(3, dz, 0), piece(0, dz, 0), x_dev))

    def forward(dz):
        into_y[dz][0].wait_recv()
        last.append(send(piece(2, dz, 0), piece(1, dz, 0), x_dev))
        into_x[dz][0].wait_recv()
        last.append(send(piece(0, dz, 1), piece(1, dz, 1), y_dev))

    outs = []

    def rescore(q0, count):
        for q in range(q0, q0 + count):
            dx, dy = QUADS[q]
            for dz in range(nz):
                copy = pltpu.make_async_copy(
                    slot(q, dz), newref_hbm.at[pl.ds(chip(dx, dy, dz) * rb, rb)],
                    out_sem.at[q * nz + dz],
                )
                copy.start()
                outs.append(copy)
        score_block(gath, q0 * qr, count * qr, width ** (-0.5))
        square_sums(gath, q0 * qr, count * qr, 1.0 / width)

    double(0, bits)
    spread(0)
    arrivals = sorted(range(1, nz), key=lambda k: (k.bit_count(), k))
    before = 0
    for dz in arrivals:
        along_z[dz].wait_recv()
        double(dz, [bit for bit in bits if bit < low[dz]])
        spread(dz)
        forward(before)
        before = dz
    forward(before)
    for dz in range(nz):
        into_y[dz][1].wait_recv()
    rescore(2, 2)
    for dz in range(nz):
        into_x[dz][1].wait_recv()
    for copy in last:
        copy.wait_recv()
    rescore(0, 2)

    high, (total,) = statistics(ITERS + 1, False)
    loglik_ref[...] = high + jnp.log(total) - math.log(rows * n_ref)
    for copy in outs:
        copy.wait()
    for copy in sent:
        copy.wait_send()


def per_device(nz, n_ref, images, references, initial_contrast):
    n, width = images.shape
    rows = references.shape[0]
    rb = rows // (4 * nz)
    qr, half = nz * rb, width // 2
    steps = ITERS + 2
    copies = steps * (n_ref - 1) + 6 * nz + 2 * (nz - 1) + (nz - 1) + 6 * nz
    peers = max(n_ref - 1, 1)
    flops = 6 * n * width * rows
    new_references, contrast, loglik = pl.pallas_call(
        functools.partial(kernel, nz, n_ref),
        out_shape=(
            pltpu.VMEM((rows, width), BF16),
            pltpu.VMEM((1, n), F32),
            pltpu.VMEM((1, n), F32),
        ),
        in_specs=[
            pl.BlockSpec(memory_space=pl.ANY),
            pl.BlockSpec(memory_space=pl.ANY),
            pl.BlockSpec(memory_space=pltpu.VMEM),
        ],
        out_specs=(
            pl.BlockSpec(memory_space=pltpu.VMEM),
            pl.BlockSpec(memory_space=pltpu.VMEM),
            pl.BlockSpec(memory_space=pltpu.VMEM),
        ),
        scratch_shapes=[
            pltpu.VMEM((n, width), BF16),
            pltpu.VMEM((rows, width), BF16),
            pltpu.VMEM((rows, LANES), F32),
            pltpu.VMEM((rows, n), F32),
            pltpu.VMEM((rows, n), BF16),
            pltpu.VMEM((4, qr, half), BF16),
            pltpu.VMEM((4, qr, half), BF16),
            pltpu.VMEM((4, qr, half), F32),
            pltpu.VMEM((2, qr, half), BF16),
            pltpu.VMEM((2, qr, half), BF16),
            pltpu.VMEM((2, max(nz - 1, 1), rb, half), BF16),
            pltpu.VMEM((2, max(nz - 1, 1), rb, half), BF16),
            pltpu.VMEM((rows, width), BF16),
            pltpu.VMEM((steps, 4, n), F32),
            pltpu.VMEM((steps * peers, 4, n), F32),
            pltpu.VMEM((8, n), F32),
            pltpu.SemaphoreType.DMA((n // LANES,)),
            pltpu.SemaphoreType.DMA((4 * nz,)),
            pltpu.SemaphoreType.DMA((4 * nz,)),
            pltpu.SemaphoreType.DMA((copies,)),
            pltpu.SemaphoreType.DMA((copies,)),
        ],
        compiler_params=pltpu.CompilerParams(
            collective_id=0, has_side_effects=True, vmem_limit_bytes=56 * 1024 * 1024
        ),
        cost_estimate=pl.CostEstimate(
            flops=flops, bytes_accessed=2 * n * width, transcendentals=0
        ),
    )(images, references, initial_contrast[None, :])
    return (new_references, contrast[0], loglik[0])


def solution(mesh):
    n_img, n_ref = mesh.shape["img"], mesh.shape["ref"]
    placed = (P("img", None), P("ref", None), P("img"))
    return jax.shard_map(
        functools.partial(per_device, n_img // 4, n_ref),
        mesh=mesh,
        in_specs=placed,
        out_specs=(P("ref", None), P("img"), P("img")),
        check_vma=False,
    )
```

```python
import functools
import math

import jax
import jax.numpy as jnp
from jax import lax
from jax.experimental import pallas as pl
from jax.experimental.pallas import tpu as pltpu
from jax.sharding import PartitionSpec as P

ITERS = 3

sharpness = 2.0
prior_weight = 1.0
epsilon = 1e-06

MESH = pl.DeviceIdType.MESH
LANES = 256
QUADS = ((1, 0), (1, 1), (0, 1), (0, 0))
F32 = jnp.float32
BF16 = jnp.bfloat16


def kernel(
    nz, n_ref, im_hbm, ref_hbm, prior_ref, newref_hbm, contrast_ref, loglik_ref,
    im, refs, norms, cross, w, snd1, rcv1, acc, snd2, rcv2, snd3, rcv3, gath,
    stat_snd, stat_rcv, vecs, im_sem, ref_sem, out_sem, ssem, rsem,
):
    n, width = im.shape
    rows = refs.shape[0]
    rb = rows // (4 * nz)
    qr = nz * rb
    half = width // 2
    me = lax.axis_index("img")
    rme = lax.axis_index("ref")
    x, y, z = lax.rem(me, 2), lax.rem(me // 2, 2), me // 4
    counter = [0]

    def chip(dx, dy, dz):
        zz, bit = z, 1
        while bit < nz:
            if dz & bit:
                zz = zz + bit - 2 * bit * lax.rem(z // bit, 2)
            bit *= 2
        return zz * 4 + lax.rem(y + dy, 2) * 2 + lax.rem(x + dx, 2)

    def send(src, dst, dev):
        i = counter[0]
        counter[0] += 1
        copy = pltpu.make_async_remote_copy(
            src_ref=src, dst_ref=dst, send_sem=ssem.at[i], recv_sem=rsem.at[i],
            device_id=dev, device_id_type=MESH,
        )
        copy.start()
        sent.append(copy)
        return copy

    sent = []
    x_dev = {"img": chip(1, 0, 0)}
    y_dev = {"img": chip(0, 1, 0)}
    z_dev = [{"img": chip(0, 0, k)} for k in range(nz)]
    r_dev = [{"ref": lax.rem(rme + k, n_ref)} for k in range(n_ref)]

    ref_copies = []
    for q, (dx, dy) in enumerate(QUADS):
        for dz in range(nz):
            s = q * nz + dz
            copy = pltpu.make_async_copy(
                ref_hbm.at[pl.ds(chip(dx, dy, dz) * rb, rb)],
                refs.at[pl.ds(s * rb, rb)], ref_sem.at[s],
            )
            copy.start()
            ref_copies.append(copy)
    im_copies = []
    for b in range(n // LANES):
        part = pl.ds(b * LANES, LANES)
        copy = pltpu.make_async_copy(im_hbm.at[part], im.at[part], im_sem.at[b])
        copy.start()
        im_copies.append(copy)

    barrier = pltpu.get_barrier_semaphore()
    peers = [x_dev, y_dev] + [z_dev[k] for k in range(1, nz) if k & (k - 1) == 0] + r_dev[1:]
    for dev in peers:
        pl.semaphore_signal(barrier, inc=1, device_id=dev, device_id_type=MESH)

    stat_snd[...] = jnp.zeros_like(stat_snd)
    vecs[0:1, :] = prior_ref[...]

    def square_sums(source, r0, count, scale):
        block = source[r0 : r0 + count, :].astype(F32)
        total = jnp.sum(block * block, axis=1, keepdims=True) * scale
        norms[r0 : r0 + count, :] = jnp.broadcast_to(total, (count, LANES))

    for s, copy in enumerate(ref_copies):
        copy.wait()
        square_sums(refs, s * rb, rb, 1.0)

    nt = (((1,), (1,)), ((), ()))
    nn = (((1,), (0,)), ((), ()))
    for copy in im_copies:
        copy.wait()

    def score_block(source, r0, count, scale):
        def body(b, carry):
            part = pl.ds(pl.multiple_of(b * LANES, LANES), LANES)
            out = lax.dot_general(
                source[r0 : r0 + count, :], im[part, :], nt, preferred_element_type=F32
            )
            cross[r0 : r0 + count, part] = out if scale is None else out * scale
            return carry

        lax.fori_loop(0, n // LANES, body, 0)

    score_block(refs, 0, rows, None)
    pl.semaphore_wait(barrier, len(peers))

    def scored(part):
        a = vecs[0:1, part]
        c = cross[:, part]
        return c, (sharpness * a) * c - ((0.5 * sharpness) * (a * a)) * norms[...]

    def statistics(it, full):
        def body(b, carry):
            part = pl.ds(pl.multiple_of(b * LANES, LANES), LANES)
            c, s = scored(part)
            top = jnp.max(s, axis=0, keepdims=True)
            e = jnp.exp(s - top)
            stat_snd[it, 0:1, part] = top
            stat_snd[it, 1:2, part] = jnp.sum(e, axis=0, keepdims=True)
            if full:
                stat_snd[it, 2:3, part] = jnp.sum(e * c, axis=0, keepdims=True)
                stat_snd[it, 3:4, part] = jnp.sum(e * norms[...], axis=0, keepdims=True)
            return carry

        lax.fori_loop(0, n // LANES, body, 0)
        copies = [
            send(stat_snd.at[it], stat_rcv.at[it * (n_ref - 1) + k - 1], r_dev[k])
            for k in range(1, n_ref)
        ]
        for copy in copies:
            copy.wait_recv()
        blocks = [stat_snd[it]] + [
            stat_rcv[it * (n_ref - 1) + k - 1] for k in range(1, n_ref)
        ]
        high = functools.reduce(jnp.maximum, [blk[0:1] for blk in blocks])
        scales = [jnp.exp(blk[0:1] - high) for blk in blocks]
        sums = [
            functools.reduce(jnp.add, [blk[j : j + 1] * sc for blk, sc in zip(blocks, scales)])
            for j in ((1, 2, 3) if full else (1,))
        ]
        return high, sums

    for it in range(ITERS):
        high, (total, along, weight) = statistics(it, True)
        vecs[0:1, :] = (along / total + prior_weight * prior_ref[...]) / (
            weight / total + prior_weight
        )
    high, (total,) = statistics(ITERS, False)
    vecs[1:2, :] = high
    vecs[2:3, :] = vecs[0:1, :] / total
    contrast_ref[...] = vecs[0:1, :]

    def weigh(b, carry):
        part = pl.ds(pl.multiple_of(b * LANES, LANES), LANES)
        _, s = scored(part)
        w[:, part] = (jnp.exp(s - vecs[1:2, part]) * vecs[2:3, part]).astype(BF16)
        return carry

    lax.fori_loop(0, n // LANES, weigh, 0)

    def weighted(r0s, c0, store):
        def body(b, carry):
            col = pl.multiple_of(b * LANES, LANES)
            lhs = [w[r0 : r0 + cnt, :] for r0, cnt in r0s]
            lhs = lhs[0] if len(lhs) == 1 else jnp.concatenate(lhs, axis=0)
            rhs = im[:, pl.ds(pl.multiple_of(c0 + col, LANES), LANES)]
            out = lax.dot_general(lhs, rhs, nn, preferred_element_type=F32)
            store(pl.ds(col, LANES), out[:qr], out[qr:])
            return carry

        lax.fori_loop(0, half // LANES, body, 0)

    def to_send(stream, first_is_far):
        def store(cols, lo, hi):
            far, near = (lo, hi) if first_is_far else (hi, lo)
            snd1[stream * 2, :, cols] = far.astype(BF16)
            snd1[stream * 2 + 1, :, cols] = near.astype(BF16)

        return store

    def to_keep(stream):
        def store(cols, lo, hi):
            acc[stream * 2, :, cols] = lo
            acc[stream * 2 + 1, :, cols] = hi

        return store

    low = [dz & -dz for dz in range(nz)]
    order = sorted(range(1, nz), key=lambda k: (low[k], -k)) + [0]
    early = [dz for dz in order if low[dz] == 1] or order
    late = [dz for dz in order if dz not in early]
    hop_dev = (x_dev, y_dev)
    step1 = {}

    def send1(s, j, dzs):
        for dz in dzs:
            part = pl.ds(dz * rb, rb)
            step1[s, j, dz] = send(
                snd1.at[s * 2 + j, part], rcv1.at[s * 2 + j, part], hop_dev[s]
            )

    weighted([(0, 2 * qr)], 0, to_send(0, False))
    send1(0, 0, early)
    send1(0, 1, early)
    weighted([(qr, 2 * qr)], half, to_send(1, True))
    send1(1, 0, early)
    send1(1, 1, early)
    weighted([(2 * qr, 2 * qr)], 0, to_keep(0))
    weighted([(0, qr), (3 * qr, qr)], half, to_keep(1))

    step2 = {}

    def send2(dzs):
        for dz in dzs:
            r0 = dz * rb
            part = pl.ds(r0, rb)
            for s in (1, 0):
                step1[s, 0, dz].wait_recv()
                snd2[s, r0 : r0 + rb, :] = (
                    acc[s * 2, r0 : r0 + rb, :] + rcv1[s * 2, r0 : r0 + rb, :].astype(F32)
                ).astype(BF16)
                step2[s, dz] = send(snd2.at[s, part], rcv2.at[s, part], hop_dev[1 - s])

    def gained(s, dz):
        step1[s, 1, dz].wait_recv()
        step2[s, dz].wait_recv()
        r0 = dz * rb
        return (
            acc[s * 2 + 1, r0 : r0 + rb, :]
            + rcv1[s * 2 + 1, r0 : r0 + rb, :].astype(F32)
            + rcv2[s, r0 : r0 + rb, :].astype(F32)
        )

    step3 = {}

    def complete(s, dz):
        total = gained(s, dz)
        for k in range(nz):
            if low[k] and k - low[k] == dz and (dz == 0 or low[k] < low[dz]):
                step3[s, k].wait_recv()
                total = total + rcv3[s, k - 1].astype(F32)
        return total

    def send3(dzs):
        for dz in dzs:
            for s in (0, 1):
                snd3[s, dz - 1] = complete(s, dz).astype(BF16)
                step3[s, dz] = send(
                    snd3.at[s, dz - 1], rcv3.at[s, dz - 1], z_dev[low[dz]]
                )

    send2(early)
    middle = [dz for dz in late if dz]
    final = [dz for dz in late if not dz]
    for j, dzs in ((0, middle), (1, middle), (0, final)):
        for s in (0, 1):
            send1(s, j, dzs)
    if late:
        send3(early)
    send2(middle)
    for s in (0, 1):
        send1(s, 1, final)
    send2(final)
    send3(middle)
    for s in (0, 1):
        acc[s * 2 + 1, 0:rb, :] = complete(s, 0)

    left, right = acc[1, 0:rb, :], acc[3, 0:rb, :]
    square = jnp.sum(left * left, axis=1, keepdims=True) + jnp.sum(
        right * right, axis=1, keepdims=True
    )
    factor = lax.rsqrt(square / width + epsilon)
    own = 3 * qr
    gath[own : own + rb, 0:half] = (left * factor).astype(BF16)
    gath[own : own + rb, half:width] = (right * factor).astype(BF16)

    def piece(q, dz, s):
        return gath.at[pl.ds(q * qr + dz * rb, rb), pl.ds(s * half, half)]

    def slot(q, dz):
        return gath.at[pl.ds(q * qr + dz * rb, rb)]

    along_z = {}

    def double(dz, bits):
        for bit in bits:
            along_z[dz + bit] = send(slot(3, dz), slot(3, dz + bit), z_dev[bit])

    bits = [1 << j for j in range(nz.bit_length() - 1)]
    into_x, into_y, last = {}, {}, []

    def spread(dz):
        into_y[dz] = [send(piece(3, dz, 0), piece(2, dz, 0), y_dev)]
        into_x[dz] = [send(piece(3, dz, 1), piece(0, dz, 1), x_dev)]
        into_y[dz].append(send(piece(3, dz, 1), piece(2, dz, 1), y_dev))
        into_x[dz].append(send(piece(3, dz, 0), piece(0, dz, 0), x_dev))

    def forward(dz):
        into_y[dz][0].wait_recv()
        last.append(send(piece(2, dz, 0), piece(1, dz, 0), x_dev))
        into_x[dz][0].wait_recv()
        last.append(send(piece(0, dz, 1), piece(1, dz, 1), y_dev))

    outs = []

    def finish(q):
        dx, dy = QUADS[q]
        for dz in range(nz):
            copy = pltpu.make_async_copy(
                slot(q, dz), newref_hbm.at[pl.ds(chip(dx, dy, dz) * rb, rb)],
                out_sem.at[q * nz + dz],
            )
            copy.start()
            outs.append(copy)
        square_sums(gath, q * qr, qr, 1.0 / width)

    double(0, bits)
    spread(0)
    arrivals = sorted(range(1, nz), key=lambda k: (k.bit_count(), k))
    before = 0
    for dz in arrivals:
        along_z[dz].wait_recv()
        double(dz, [bit for bit in bits if bit < low[dz]])
        spread(dz)
        forward(before)
        before = dz
    forward(before)
    for dz in range(nz):
        into_y[dz][1].wait_recv()
    finish(3)
    finish(2)
    score_block(gath, 2 * qr, 2 * qr, width ** (-0.5))
    for dz in range(nz):
        into_x[dz][1].wait_recv()
    finish(0)
    for copy in last:
        copy.wait_recv()
    finish(1)
    score_block(gath, 0, 2 * qr, width ** (-0.5))

    high, (total,) = statistics(ITERS + 1, False)
    loglik_ref[...] = high + jnp.log(total) - math.log(rows * n_ref)
    for copy in outs:
        copy.wait()
    for copy in sent:
        copy.wait_send()


def per_device(nz, n_ref, images, references, initial_contrast):
    n, width = images.shape
    rows = references.shape[0]
    rb = rows // (4 * nz)
    qr, half = nz * rb, width // 2
    steps = ITERS + 2
    copies = steps * (n_ref - 1) + 6 * nz + 2 * (nz - 1) + (nz - 1) + 6 * nz
    peers = max(n_ref - 1, 1)
    flops = 6 * n * width * rows
    new_references, contrast, loglik = pl.pallas_call(
        functools.partial(kernel, nz, n_ref),
        out_shape=(
            pltpu.VMEM((rows, width), BF16),
            pltpu.VMEM((1, n), F32),
            pltpu.VMEM((1, n), F32),
        ),
        in_specs=[
            pl.BlockSpec(memory_space=pl.ANY),
            pl.BlockSpec(memory_space=pl.ANY),
            pl.BlockSpec(memory_space=pltpu.VMEM),
        ],
        out_specs=(
            pl.BlockSpec(memory_space=pltpu.VMEM),
            pl.BlockSpec(memory_space=pltpu.VMEM),
            pl.BlockSpec(memory_space=pltpu.VMEM),
        ),
        scratch_shapes=[
            pltpu.VMEM((n, width), BF16),
            pltpu.VMEM((rows, width), BF16),
            pltpu.VMEM((rows, LANES), F32),
            pltpu.VMEM((rows, n), F32),
            pltpu.VMEM((rows, n), BF16),
            pltpu.VMEM((4, qr, half), BF16),
            pltpu.VMEM((4, qr, half), BF16),
            pltpu.VMEM((4, qr, half), F32),
            pltpu.VMEM((2, qr, half), BF16),
            pltpu.VMEM((2, qr, half), BF16),
            pltpu.VMEM((2, max(nz - 1, 1), rb, half), BF16),
            pltpu.VMEM((2, max(nz - 1, 1), rb, half), BF16),
            pltpu.VMEM((rows, width), BF16),
            pltpu.VMEM((steps, 4, n), F32),
            pltpu.VMEM((steps * peers, 4, n), F32),
            pltpu.VMEM((8, n), F32),
            pltpu.SemaphoreType.DMA((n // LANES,)),
            pltpu.SemaphoreType.DMA((4 * nz,)),
            pltpu.SemaphoreType.DMA((4 * nz,)),
            pltpu.SemaphoreType.DMA((copies,)),
            pltpu.SemaphoreType.DMA((copies,)),
        ],
        compiler_params=pltpu.CompilerParams(
            collective_id=0, has_side_effects=True, vmem_limit_bytes=56 * 1024 * 1024
        ),
        cost_estimate=pl.CostEstimate(
            flops=flops, bytes_accessed=2 * n * width, transcendentals=0
        ),
    )(images, references, initial_contrast[None, :])
    return (new_references, contrast[0], loglik[0])


def solution(mesh):
    n_img, n_ref = mesh.shape["img"], mesh.shape["ref"]
    placed = (P("img", None), P("ref", None), P("img"))
    return jax.shard_map(
        functools.partial(per_device, n_img // 4, n_ref),
        mesh=mesh,
        in_specs=placed,
        out_specs=(P("ref", None), P("img"), P("img")),
        check_vma=False,
    )
```
